32 devices in a mesh: grp: 2 (over y), samp: 4 (over z), snp: 4 (over x, core).
Axes of the slice: x: 2, y: 2, z: 4, core: 2. Of those that a mesh axis runs over, the one named last changes fastest.
Arguments:
- genotypes: int32 [2048, 8192], P(('grp', 'samp'), 'snp'), parts along dimension 0, may hold values from 0 to 2730, as said below
- basis_cols: bfloat16 [16384, 256], P(('grp', 'snp')), parts along dimension 0, may hold values from -0.0625 to 0.0625
Outputs:
- y_block: float32 [8, 4, 512, 256], P(('grp', 'snp'), 'samp'), parts along dimension 0
- r_factor: float32 [512, 256], P('grp'), parts along dimension 0
- q_next: float32 [8, 4, 512, 256], P(('grp', 'snp'), 'samp'), parts along dimension 0
The draws below stay inside these ranges and needn't reach their ends.
There are 2 independent parts, one for each index of `grp`. The reference program is written for one: setup_inputs(seed, part) draws one part's arguments, and reference() takes and returns one part's arrays. A program takes and returns all parts, laid end to end along the dimension named above; each array names one. Nothing has to cross between parts.
Inputs may be any that keep to these rules, and one draw needn't show every extreme that they name: `genotypes`: each word packs 6 dosages of 0, 1 or 2 in pairs of bits: bits 2 t and 2 t + 1 of word (w, p) hold the dosage of sample 6 w + t at SNP p, t from 0 to 5; bits 12 and up are zero.
All inputs are finite; a program needn't handle non-finite values.
Results may differ from the reference program's by a relative error of at most 0.0025.
Values may be sent and summed in bfloat16 or wider, within the bound.
A program may use at most 64 MiB of HBM per device.

```python
import math
import jax
import jax.numpy as jnp
from jax import lax

K = 256
PD = 2048
WD = 256
NP = 8192
N_SAMP = 4
N_SNP = 4


def draw_genotypes(key, part):
    key_base = jax.random.fold_in(key, 11)
    key_drift = jax.random.fold_in(key, 12)
    key_dose = jax.random.fold_in(key, 13)
    word_count = WD * N_SAMP
    snp_count = PD * N_SNP
    base_freq = jax.random.randint(key_base, (snp_count,), 10, 91)
    drift_level = jax.random.randint(key_drift, (N_SAMP, snp_count), 0, 3)
    frequency = base_freq[None, :] * (1 + drift_level) // 3
    freq_rows = jnp.repeat(frequency, WD, axis=0)
    packed = jnp.zeros((word_count, snp_count), jnp.int32)
    for plane_idx in range(6):
        plane_key = jax.random.fold_in(key_dose, plane_idx)
        first_draw = jax.random.randint(jax.random.fold_in(plane_key, 1), (word_count, snp_count), 0, 100)
        second_draw = jax.random.randint(jax.random.fold_in(plane_key, 2), (word_count, snp_count), 0, 100)
        dose_plane = (first_draw < freq_rows).astype(jnp.int32) + (second_draw < freq_rows).astype(jnp.int32)
        packed = packed + dose_plane * 4 ** plane_idx
    return packed


def levels(own_key, dims, pieces, least, top_value):
    level = 1.0
    for dim, parts in pieces:
        heights = jax.random.uniform(jax.random.fold_in(jax.random.fold_in(own_key, 6), dim), (parts,), jnp.float32, least / len(pieces), top_value / len(pieces))
        level = level * jnp.repeat(jnp.exp(heights), dims[dim] // parts).reshape((-1,) + (1,) * (len(dims) - 1 - dim))
    return level


def scatter_about(own_key, dims, deviation, reach, cuts=(), held_as=jnp.bfloat16):
    loudness = levels(own_key, dims, cuts, -0.22, 0.18) if cuts else 1.0
    drawn = jax.random.normal(own_key, dims, jnp.float32) * deviation * loudness
    return jnp.minimum(jnp.maximum(drawn, -reach), reach).astype(held_as)


def setup_inputs(seed: int = 0, part: int = 0) -> dict:
    arg_keys = jax.random.split(jax.random.key(seed), 3)
    part_keys = jax.random.split(jax.random.fold_in(arg_keys[2], part), 3)
    genotypes = draw_genotypes(jax.random.fold_in(jax.random.fold_in(arg_keys[2], part), 71), part)
    basis_cols = scatter_about(part_keys[1], (NP, K), NP ** -0.5, 0.0625, ((0, 4),))
    return {"genotypes": genotypes, "basis_cols": basis_cols}


def unpack(word_block):
    planes = [jnp.bitwise_and(jnp.right_shift(word_block, 2 * shift_pos), 3) for shift_pos in range(6)]
    return jnp.stack(planes, axis=1).reshape(word_block.shape[0] * 6, word_block.shape[1])

def reference(genotypes, basis_cols):
    word_count, snp_count = genotypes.shape
    samples = word_count * 6
    block_words = math.gcd(word_count, 64)
    blocks = genotypes.reshape(word_count // block_words, block_words, snp_count)

    def count_block(running, word_block):
        return (running + lax.optimization_barrier(jnp.sum(unpack(word_block), axis=0)).astype(jnp.int32), None)
    counts, unused = lax.scan(count_block, jnp.zeros((snp_count,), jnp.int32), blocks)
    allele_mean = counts.astype(jnp.float32) / jnp.float32(samples)
    center = jnp.dot(allele_mean, basis_cols.astype(jnp.float32), precision=lax.Precision.HIGHEST)

    def project_block(running, word_block):
        dosage = unpack(word_block).astype(jnp.bfloat16)
        scores = (jnp.dot(dosage.astype(jnp.float32), basis_cols.astype(jnp.float32), preferred_element_type=jnp.float32) - center[None, :]).astype(jnp.bfloat16)
        return (running + lax.dot_general(dosage.astype(jnp.float32), scores.astype(jnp.float32), (((0,), (0,)), ((), ())), preferred_element_type=jnp.float32), None)
    y_full, unused = lax.scan(project_block, jnp.zeros((snp_count, basis_cols.shape[1]), jnp.float32), blocks)
    y_full = y_full * (jnp.float32(1.0) / jnp.sqrt(jnp.float32(samples)))
    gram_sum = jnp.dot(y_full.T, y_full, precision=lax.Precision.HIGHEST) / jnp.float32(snp_count)
    lower_factor = jnp.linalg.cholesky(gram_sum)
    q_next = lax.linalg.triangular_solve(lower_factor, y_full, left_side=False, lower=True, transpose_a=True)
    layout = (N_SNP, N_SAMP, snp_count // (N_SNP * N_SAMP), basis_cols.shape[1])
    return (y_full.reshape(layout), lower_factor.T, q_next.reshape(layout))
```

```python
import functools
import jax
import jax.numpy as jnp
from jax import lax
from jax.experimental import pallas as pl
from jax.experimental.pallas import tpu as pltpu
from jax.sharding import PartitionSpec as P

PLANES = 6
MESH = pl.DeviceIdType.MESH
F32 = jnp.float32
BF16 = jnp.bfloat16
HIGH = lax.Precision.HIGHEST
LEVELS = 32767.0


def log2(n):
    bits = n.bit_length() - 1
    assert 1 << bits == n
    return bits


def segments(me, bits, rows):
    base, steps = 0, []
    for b in range(bits):
        bit = (me // (1 << b)) % 2
        half = rows >> (b + 1)
        steps.append((base + bit * half, base + (1 - bit) * half, half))
        base = base + bit * half
    return steps


def main_kernel(
    n_snp, n_samp, chunks,
    g_ref, b_ref, y_ref, gram_ref,
    part, rs_rx, scores, dose_t, cs_tx, cs_rx, ct_tx, ct_rx,
    yq, ysc, yq_rx, ysc_rx, gwork, g_rx, gs_rx, gout,
    rs_s, rs_r, ag_s, ag_r, cs_s, cs_r, ct_s, ct_r, yq_s, yq_r, ysc_s, ysc_r,
    gr_s, gr_r, gs_s, gs_r, ga_s, ga_r,
):
    snp, samp = lax.axis_index("snp"), lax.axis_index("samp")
    bits = log2(n_snp)
    words = g_ref.shape[0]
    rows = PLANES * words
    width = b_ref.shape[1]
    crow = rows // chunks
    samples = rows * n_samp

    def copy(src, dst, ssem, rsem, axis, peer):
        return pltpu.make_async_remote_copy(
            src_ref=src, dst_ref=dst, send_sem=ssem, recv_sem=rsem,
            device_id={axis: peer}, device_id_type=MESH,
        )

    def partner(b):
        bit = (snp // (1 << b)) % 2
        return snp + (1 - 2 * bit) * (1 << b)

    barrier = pltpu.get_barrier_semaphore()
    for d in range(1, n_snp):
        pl.semaphore_signal(barrier, inc=1, device_id={"snp": lax.rem(snp + d, n_snp)}, device_id_type=MESH)
    for d in range(1, n_samp):
        pl.semaphore_signal(barrier, inc=1, device_id={"samp": lax.rem(samp + d, n_samp)}, device_id_type=MESH)

    steps = segments(snp, bits, crow)

    def rows_at(c, off, size):
        return pl.ds(pl.multiple_of(c * crow + off, 16), size)

    def rs_copy(c, b):
        keep, send, half = steps[b]
        return copy(
            part.at[rows_at(c, send, half)],
            rs_rx.at[pl.ds(c * crow + crow - 2 * half, half)],
            rs_s.at[c, b], rs_r.at[c, b], "snp", partner(b),
        )

    def ag_copy(c, b):
        keep, send, half = steps[b]
        seg = rows_at(c, keep, half)
        return copy(scores.at[seg], scores.at[seg], ag_s.at[c, b], ag_r.at[c, b], "snp", partner(b))

    per = PLANES // chunks
    colsum = jnp.zeros((8, width), F32)
    for c in range(chunks):
        for t in range(c * per, (c + 1) * per):
            dose = ((g_ref[...] >> (2 * t)) & 3).astype(F32).astype(BF16)
            prod = jnp.dot(dose, b_ref[...], preferred_element_type=F32)
            part[pl.ds(t * words, words), :] = prod
            colsum = colsum + prod.reshape(words // 8, 8, width).sum(axis=0)
        if c == 0:
            pl.semaphore_wait(barrier, n_snp + n_samp - 2)
        rs_copy(c, 0).start()
    cs_tx[...] = colsum

    def cs_copy(d):
        return copy(cs_tx, cs_rx.at[d], cs_s.at[d], cs_r.at[d], "snp", lax.rem(snp + d, n_snp))

    def ct_copy(d):
        return copy(ct_tx, ct_rx.at[d], ct_s.at[d], ct_r.at[d], "samp", lax.rem(samp + d, n_samp))

    for d in range(1, n_snp):
        cs_copy(d).start()

    def reduce_step(b, center=None):
        for c in range(chunks):
            keep, send, half = steps[b]
            rs_copy(c, b).wait()
            seg = rows_at(c, keep, half)
            total = part[seg, :] + rs_rx[pl.ds(c * crow + crow - 2 * half, half), :]
            if b + 1 < bits:
                part[seg, :] = total
                rs_copy(c, b + 1).start()
            else:
                scores[seg, :] = (total - center).astype(BF16)
                ag_copy(c, b).start()

    for b in range(bits - 1):
        reduce_step(b)
        if b == 0:
            tot = colsum
            for d in range(1, n_snp):
                cs_copy(d).wait()
                tot = tot + cs_rx[d]
            ct_tx[...] = tot
            for d in range(1, n_samp):
                ct_copy(d).start()
    word_t = g_ref[...].T
    for t in range(PLANES):
        dose_t[:, t * words:(t + 1) * words] = ((word_t >> (2 * t)) & 3).astype(F32).astype(BF16)
    for d in range(1, n_samp):
        ct_copy(d).wait()
        tot = tot + ct_rx[d]
    center = tot.sum(axis=0, keepdims=True) / F32(samples)
    reduce_step(bits - 1, center)
    for b in range(bits - 1, -1, -1):
        for c in range(chunks):
            ag_copy(c, b).wait()
            if b:
                ag_copy(c, b - 1).start()

    inv_root = F32(1.0) / jnp.sqrt(F32(samples))
    own_rows = y_ref.shape[0]

    def y_part(owner):
        blk = dose_t[pl.ds(pl.multiple_of(owner * own_rows, 16), own_rows), :]
        return jnp.dot(blk, scores[...], preferred_element_type=F32) * inv_root

    def y_copies(d):
        to = lax.rem(samp + d, n_samp)
        return (
            copy(yq.at[d], yq_rx.at[d], yq_s.at[d], yq_r.at[d], "samp", to),
            copy(ysc.at[d], ysc_rx.at[d], ysc_s.at[d], ysc_r.at[d], "samp", to),
        )

    for d in range(1, n_samp):
        block = y_part(lax.rem(samp + d, n_samp))
        top = jnp.maximum(jnp.max(jnp.abs(block), axis=0, keepdims=True), F32(1e-30))
        yq[d] = jnp.round(block * (F32(LEVELS) / top)).astype(jnp.int32).astype(jnp.int16)
        ysc[d] = jnp.broadcast_to(top * F32(1.0 / LEVELS), (8, width))
        for cp in y_copies(d):
            cp.start()
    y = y_part(samp)
    for d in range(1, n_samp):
        for cp in y_copies(d):
            cp.wait()
        y = y + yq_rx[d].astype(jnp.int32).astype(F32) * ysc_rx[d][0:1, :]
    y_ref[...] = y

    snp_total = dose_t.shape[0] * n_snp
    gwork[...] = lax.dot_general(y, y, (((0,), (0,)), ((), ())), precision=HIGH, preferred_element_type=F32) / F32(snp_total)
    gsteps = segments(snp, bits, width)

    def at(off, size):
        return pl.ds(pl.multiple_of(off, 8), size)

    def gr_copy(b):
        keep, send, half = gsteps[b]
        return copy(gwork.at[at(send, half)], g_rx.at[pl.ds(width - 2 * half, half)], gr_s.at[b], gr_r.at[b], "snp", partner(b))

    def ga_copy(b):
        keep, send, half = gsteps[b]
        return copy(gout.at[at(keep, half)], gout.at[at(keep, half)], ga_s.at[b], ga_r.at[b], "snp", partner(b))

    for b in range(bits):
        keep, send, half = gsteps[b]
        gr_copy(b).start()
        gr_copy(b).wait()
        mine = gwork[at(keep, half), :] + g_rx[pl.ds(width - 2 * half, half), :]
        gwork[at(keep, half), :] = mine
    keep, send, half = gsteps[bits - 1]

    def gs_copy(d):
        return copy(gwork.at[at(keep, half)], gs_rx.at[samp], gs_s.at[d], gs_r.at[d], "samp", lax.rem(samp + d, n_samp))

    for d in range(1, n_samp):
        gs_copy(d).start()
    gs_rx[samp] = mine
    for d in range(1, n_samp):
        gs_copy(d).wait()
    total = gs_rx[0]
    for j in range(1, n_samp):
        total = total + gs_rx[j]
    gout[at(keep, half), :] = total
    for b in range(bits - 1, -1, -1):
        ga_copy(b).start()
        ga_copy(b).wait()
    gram_ref[...] = gout[...]


def eliminate(a):
    n = a.shape[0]
    groups = n // 8
    lane = lax.broadcasted_iota(jnp.int32, (8, n), 1)
    sub = lax.broadcasted_iota(jnp.int32, (8, n), 0)
    left = [a[8 * g:8 * g + 8, :] for g in range(groups)]
    right = [jnp.where(lane == sub + 8 * g, F32(1.0), F32(0.0)) for g in range(groups)]
    for j in range(n):
        g0, s = j // 8, j % 8
        row = left[g0][s:s + 1, :]
        inv = F32(1.0) / row[:, j:j + 1]
        row_l = row * inv
        row_r = right[g0][s:s + 1, :] * inv
        for g in range(g0, groups):
            if g == g0 and s == 7:
                continue
            col = jnp.broadcast_to(left[g][:, j:j + 1], (8, n))
            if g == g0:
                col = jnp.where(sub > s, col, F32(0.0))
            left[g] = left[g] - col * row_l
            right[g] = right[g] - col * row_r
    ups, invs = [], []
    for g in range(groups):
        diag = jnp.sum(jnp.where(lane == sub + 8 * g, left[g], F32(0.0)), axis=1, keepdims=True)
        scale = F32(1.0) / jnp.sqrt(diag)
        ups.append(jnp.where(lane >= sub + 8 * g, left[g] * scale, F32(0.0)))
        invs.append(right[g] * scale)
    return jnp.concatenate(ups, axis=0), jnp.concatenate(invs, axis=0)


def factor_kernel(gram_ref, y_ref, r_ref, q_ref, inv_ref):
    width = gram_ref.shape[0]
    nb = min(128, width)
    blocks = width // nb

    def blk(ref, i, j):
        return ref[i * nb:(i + 1) * nb, j * nb:(j + 1) * nb]

    def dot(a, b, dims):
        return lax.dot_general(a, b, (dims, ((), ())), precision=HIGH, preferred_element_type=F32)

    r_ref[...] = jnp.zeros_like(r_ref)
    inv_ref[...] = jnp.zeros_like(inv_ref)
    for k in range(blocks):
        a = blk(gram_ref, k, k)
        for m in range(k):
            a = a - dot(blk(r_ref, m, k), blk(r_ref, m, k), ((0,), (0,)))
        upper, inv = eliminate(a)
        r_ref[k * nb:(k + 1) * nb, k * nb:(k + 1) * nb] = upper
        inv_ref[k * nb:(k + 1) * nb, k * nb:(k + 1) * nb] = inv
        for j in range(k + 1, blocks):
            a = blk(gram_ref, k, j)
            for m in range(k):
                a = a - dot(blk(r_ref, m, k), blk(r_ref, m, j), ((0,), (0,)))
            r_ref[k * nb:(k + 1) * nb, j * nb:(j + 1) * nb] = dot(inv, a, ((1,), (0,)))
        for j in range(k):
            acc = jnp.zeros((nb, nb), F32)
            for m in range(j, k):
                acc = acc + dot(blk(r_ref, m, k), blk(inv_ref, m, j), ((0,), (0,)))
            inv_ref[k * nb:(k + 1) * nb, j * nb:(j + 1) * nb] = -dot(inv, acc, ((1,), (0,)))
    q_ref[...] = dot(y_ref[...], inv_ref[...], ((1,), (1,)))


def per_device(n_snp, n_samp, genotypes, basis_cols):
    words, snps = genotypes.shape
    width = basis_cols.shape[1]
    rows = PLANES * words
    chunks = 3
    own = snps // n_samp
    bits = log2(n_snp)
    vmem = pl.BlockSpec(memory_space=pltpu.VMEM)
    dma = pltpu.SemaphoreType.DMA
    y, gram = pl.pallas_call(
        functools.partial(main_kernel, n_snp, n_samp, chunks),
        out_shape=(
            jax.ShapeDtypeStruct((own, width), F32),
            jax.ShapeDtypeStruct((width, width), F32),
        ),
        in_specs=[vmem, vmem],
        out_specs=(vmem, vmem),
        scratch_shapes=[
            pltpu.VMEM((rows, width), F32),
            pltpu.VMEM((rows, width), F32),
            pltpu.VMEM((rows, width), BF16),
            pltpu.VMEM((snps, rows), BF16),
            pltpu.VMEM((8, width), F32),
            pltpu.VMEM((n_snp, 8, width), F32),
            pltpu.VMEM((8, width), F32),
            pltpu.VMEM((n_samp, 8, width), F32),
            pltpu.VMEM((n_samp, own, width), jnp.int16),
            pltpu.VMEM((n_samp, 8, width), F32),
            pltpu.VMEM((n_samp, own, width), jnp.int16),
            pltpu.VMEM((n_samp, 8, width), F32),
            pltpu.VMEM((width, width), F32),
            pltpu.VMEM((width, width), F32),
            pltpu.VMEM((n_samp, width // n_snp, width), F32),
            pltpu.VMEM((width, width), F32),
            dma((chunks, bits)), dma((chunks, bits)), dma((chunks, bits)), dma((chunks, bits)),
            dma((n_snp,)), dma((n_snp,)), dma((n_samp,)), dma((n_samp,)),
            dma((n_samp,)), dma((n_samp,)), dma((n_samp,)), dma((n_samp,)),
            dma((bits,)), dma((bits,)), dma((n_samp,)), dma((n_samp,)), dma((bits,)), dma((bits,)),
        ],
        compiler_params=pltpu.CompilerParams(collective_id=0, has_side_effects=True),
    )(genotypes, basis_cols)
    r_factor, q_next = pl.pallas_call(
        factor_kernel,
        out_shape=(
            jax.ShapeDtypeStruct((width, width), F32),
            jax.ShapeDtypeStruct((own, width), F32),
        ),
        in_specs=[vmem, vmem],
        out_specs=(vmem, vmem),
        scratch_shapes=[pltpu.VMEM((width, width), F32)],
    )(gram, y)
    layout = (1, 1, own, width)
    return (y.reshape(layout), r_factor, q_next.reshape(layout))


def solution(mesh):
    return jax.shard_map(
        functools.partial(per_device, mesh.shape["snp"], mesh.shape["samp"]),
        mesh=mesh,
        in_specs=(P(("grp", "samp"), "snp"), P(("grp", "snp"), None)),
        out_specs=(
            P(("grp", "snp"), "samp", None, None),
            P("grp", None),
            P(("grp", "snp"), "samp", None, None),
        ),
        check_vma=False,
    )
```

```python
import functools
import jax
import jax.numpy as jnp
from jax import lax
from jax.experimental import pallas as pl
from jax.experimental.pallas import tpu as pltpu
from jax.sharding import PartitionSpec as P

PLANES = 6
MESH = pl.DeviceIdType.MESH
F32 = jnp.float32
BF16 = jnp.bfloat16
HIGH = lax.Precision.HIGHEST
LEVELS = 32767.0


def log2(n):
    bits = n.bit_length() - 1
    assert 1 << bits == n
    return bits


def segments(me, bits, rows):
    base, steps = 0, []
    for b in range(bits):
        bit = (me // (1 << b)) % 2
        half = rows >> (b + 1)
        steps.append((base + bit * half, base + (1 - bit) * half, half))
        base = base + bit * half
    return steps


def main_kernel(
    n_snp, n_samp, chunks,
    g_ref, b_ref, y_ref, gram_ref,
    part, rs_rx, scores, dose_t, cs_tx, cs_rx, ct_tx, ct_rx,
    yq, ysc, yq_rx, ysc_rx, gwork, g_rx, gs_rx, gout,
    rs_s, rs_r, ag_s, ag_r, cs_s, cs_r, ct_s, ct_r, yq_s, yq_r, ysc_s, ysc_r,
    gr_s, gr_r, gs_s, gs_r, ga_s, ga_r,
):
    snp, samp = lax.axis_index("snp"), lax.axis_index("samp")
    bits = log2(n_snp)
    words = g_ref.shape[0]
    rows = PLANES * words
    width = b_ref.shape[1]
    crow = rows // chunks
    samples = rows * n_samp

    def copy(src, dst, ssem, rsem, axis, peer):
        return pltpu.make_async_remote_copy(
            src_ref=src, dst_ref=dst, send_sem=ssem, recv_sem=rsem,
            device_id={axis: peer}, device_id_type=MESH,
        )

    def partner(b):
        bit = (snp // (1 << b)) % 2
        return snp + (1 - 2 * bit) * (1 << b)

    barrier = pltpu.get_barrier_semaphore()
    for d in range(1, n_snp):
        pl.semaphore_signal(barrier, inc=1, device_id={"snp": lax.rem(snp + d, n_snp)}, device_id_type=MESH)
    for d in range(1, n_samp):
        pl.semaphore_signal(barrier, inc=1, device_id={"samp": lax.rem(samp + d, n_samp)}, device_id_type=MESH)

    steps = segments(snp, bits, crow)

    def rows_at(c, off, size):
        return pl.ds(pl.multiple_of(c * crow + off, 16), size)

    def rs_copy(c, b):
        keep, send, half = steps[b]
        return copy(
            part.at[rows_at(c, send, half)],
            rs_rx.at[pl.ds(c * crow + crow - 2 * half, half)],
            rs_s.at[c, b], rs_r.at[c, b], "snp", partner(b),
        )

    def ag_copy(c, b):
        keep, send, half = steps[b]
        seg = rows_at(c, keep, half)
        return copy(scores.at[seg], scores.at[seg], ag_s.at[c, b], ag_r.at[c, b], "snp", partner(b))

    per = PLANES // chunks
    colsum = jnp.zeros((8, width), F32)
    for c in range(chunks):
        for t in range(c * per, (c + 1) * per):
            dose = ((g_ref[...] >> (2 * t)) & 3).astype(F32).astype(BF16)
            prod = jnp.dot(dose, b_ref[...], preferred_element_type=F32)
            part[pl.ds(t * words, words), :] = prod
            colsum = colsum + prod.reshape(words // 8, 8, width).sum(axis=0)
        if c == 0:
            pl.semaphore_wait(barrier, n_snp + n_samp - 2)
        rs_copy(c, 0).start()
    cs_tx[...] = colsum

    def cs_copy(d):
        return copy(cs_tx, cs_rx.at[d], cs_s.at[d], cs_r.at[d], "snp", lax.rem(snp + d, n_snp))

    def ct_copy(d):
        return copy(ct_tx, ct_rx.at[d], ct_s.at[d], ct_r.at[d], "samp", lax.rem(samp + d, n_samp))

    for d in range(1, n_snp):
        cs_copy(d).start()

    def reduce_step(b, center=None):
        for c in range(chunks):
            keep, send, half = steps[b]
            rs_copy(c, b).wait()
            seg = rows_at(c, keep, half)
            total = part[seg, :] + rs_rx[pl.ds(c * crow + crow - 2 * half, half), :]
            if b + 1 < bits:
                part[seg, :] = total
                rs_copy(c, b + 1).start()
            else:
                scores[seg, :] = (total - center).astype(BF16)
                ag_copy(c, b).start()

    for b in range(bits - 1):
        reduce_step(b)
        if b == 0:
            tot = colsum
            for d in range(1, n_snp):
                cs_copy(d).wait()
                tot = tot + cs_rx[d]
            ct_tx[...] = tot
            for d in range(1, n_samp):
                ct_copy(d).start()
    word_t = g_ref[...].T
    for t in range(PLANES):
        dose_t[:, t * words:(t + 1) * words] = ((word_t >> (2 * t)) & 3).astype(F32).astype(BF16)
    for d in range(1, n_samp):
        ct_copy(d).wait()
        tot = tot + ct_rx[d]
    center = tot.sum(axis=0, keepdims=True) / F32(samples)
    reduce_step(bits - 1, center)
    for b in range(bits - 1, -1, -1):
        for c in range(chunks):
            ag_copy(c, b).wait()
            if b:
                ag_copy(c, b - 1).start()

    inv_root = F32(1.0) / jnp.sqrt(F32(samples))
    own_rows = y_ref.shape[0]

    def y_part(owner):
        blk = dose_t[pl.ds(pl.multiple_of(owner * own_rows, 16), own_rows), :]
        return jnp.dot(blk, scores[...], preferred_element_type=F32) * inv_root

    def y_copies(d):
        to = lax.rem(samp + d, n_samp)
        return (
            copy(yq.at[d], yq_rx.at[d], yq_s.at[d], yq_r.at[d], "samp", to),
            copy(ysc.at[d], ysc_rx.at[d], ysc_s.at[d], ysc_r.at[d], "samp", to),
        )

    for d in range(1, n_samp):
        block = y_part(lax.rem(samp + d, n_samp))
        top = jnp.maximum(jnp.max(jnp.abs(block), axis=0, keepdims=True), F32(1e-30))
        yq[d] = jnp.round(block * (F32(LEVELS) / top)).astype(jnp.int32).astype(jnp.int16)
        ysc[d] = jnp.broadcast_to(top * F32(1.0 / LEVELS), (8, width))
        for cp in y_copies(d):
            cp.start()
    y = y_part(samp)
    for d in range(1, n_samp):
        for cp in y_copies(d):
            cp.wait()
        y = y + yq_rx[d].astype(jnp.int32).astype(F32) * ysc_rx[d][0:1, :]
    y_ref[...] = y

    snp_total = dose_t.shape[0] * n_snp
    half_w = width // 2
    packed = width - width // 4
    top = lax.dot_general(y[:, :half_w], y, (((0,), (0,)), ((), ())), precision=HIGH, preferred_element_type=F32)
    low = lax.dot_general(y[:, half_w:], y[:, half_w:], (((0,), (0,)), ((), ())), precision=HIGH, preferred_element_type=F32)
    gwork[:half_w, :] = top / F32(snp_total)
    gwork[half_w:, :half_w] = low[:half_w // 2, :] / F32(snp_total)
    gwork[half_w:, half_w:] = low[half_w // 2:, :] / F32(snp_total)
    gsteps = segments(snp, bits, packed)

    def at(off, size):
        return pl.ds(pl.multiple_of(off, 8), size)

    def gr_copy(b):
        keep, send, half = gsteps[b]
        return copy(gwork.at[at(send, half)], g_rx.at[pl.ds(packed - 2 * half, half)], gr_s.at[b], gr_r.at[b], "snp", partner(b))

    def ga_copy(b):
        keep, send, half = gsteps[b]
        return copy(gout.at[at(keep, half)], gout.at[at(keep, half)], ga_s.at[b], ga_r.at[b], "snp", partner(b))

    for b in range(bits):
        keep, send, half = gsteps[b]
        gr_copy(b).start()
        gr_copy(b).wait()
        mine = gwork[at(keep, half), :] + g_rx[pl.ds(packed - 2 * half, half), :]
        gwork[at(keep, half), :] = mine
    keep, send, half = gsteps[bits - 1]

    def gs_copy(d):
        return copy(gwork.at[at(keep, half)], gs_rx.at[samp], gs_s.at[d], gs_r.at[d], "samp", lax.rem(samp + d, n_samp))

    for d in range(1, n_samp):
        gs_copy(d).start()
    gs_rx[samp] = mine
    for d in range(1, n_samp):
        gs_copy(d).wait()
    total = gs_rx[0]
    for j in range(1, n_samp):
        total = total + gs_rx[j]
    gout[at(keep, half), :] = total
    for b in range(bits - 1, -1, -1):
        ga_copy(b).start()
        ga_copy(b).wait()
    gram_ref[:half_w, :] = gout[:half_w, :]
    gram_ref[half_w:half_w + half_w // 2, half_w:] = gout[half_w:, :half_w]
    gram_ref[half_w + half_w // 2:, half_w:] = gout[half_w:, half_w:]
    gram_ref[half_w:, :half_w] = jnp.zeros((half_w, half_w), F32)


def eliminate(a):
    n = a.shape[0]
    groups = n // 8
    lane = lax.broadcasted_iota(jnp.int32, (8, n), 1)
    sub = lax.broadcasted_iota(jnp.int32, (8, n), 0)
    left = [a[8 * g:8 * g + 8, :] for g in range(groups)]
    right = [jnp.where(lane == sub + 8 * g, F32(1.0), F32(0.0)) for g in range(groups)]

    def across(x, j):
        return jnp.broadcast_to(x[:, j:j + 1], (8, n))

    def down(x, s):
        return jnp.broadcast_to(x[s:s + 1, :], (8, n))

    for p in range(0, n, 2):
        g0, s = p // 8, p % 8
        cu, cv = across(left[g0], p), across(left[g0], p + 1)
        a00, a10, a11 = down(cu, s), down(cu, s + 1), down(cv, s + 1)
        inv_a = F32(1.0) / a00
        inv_det = F32(1.0) / (a00 * a11 - a10 * a10)
        m = a10 * inv_a
        f = a00 * inv_det
        u, v = down(left[g0], s), down(left[g0], s + 1)
        ur, vr = down(right[g0], s), down(right[g0], s + 1)
        ul, url = u * inv_a, ur * inv_a
        vl, vrl = (v - m * u) * f, (vr - m * ur) * f
        for g in range(g0, groups):
            if g > g0:
                cu, cv = across(left[g], p), across(left[g], p + 1)
            c0, c1 = cu, cv - cu * m
            if g == g0:
                c0 = jnp.where(sub > s, c0, F32(0.0))
                c1 = jnp.where(sub > s + 1, c1, F32(0.0))
            left[g] = left[g] - c0 * ul - c1 * vl
            right[g] = right[g] - c0 * url - c1 * vrl
    ups, invs = [], []
    for g in range(groups):
        diag = jnp.sum(jnp.where(lane == sub + 8 * g, left[g], F32(0.0)), axis=1, keepdims=True)
        scale = F32(1.0) / jnp.sqrt(diag)
        ups.append(jnp.where(lane >= sub + 8 * g, left[g] * scale, F32(0.0)))
        invs.append(right[g] * scale)
    return jnp.concatenate(ups, axis=0), jnp.concatenate(invs, axis=0)


def factor_kernel(gram_in, y_ref, y_out, r_ref, q_ref, inv_ref, gram_ref, y_sem):
    y_copy = pltpu.make_async_copy(y_ref, y_out, y_sem)
    y_copy.start()
    width = gram_in.shape[0]
    on = lax.broadcasted_iota(jnp.int32, (width, width), 0) == lax.broadcasted_iota(jnp.int32, (width, width), 1)
    kept = jnp.where(on, gram_in[...], F32(0.0))
    d_row = jnp.sqrt(jnp.sum(kept, axis=0, keepdims=True))
    d_col = jnp.sqrt(jnp.sum(kept, axis=1, keepdims=True))
    gram_ref[...] = gram_in[...] * (F32(1.0) / d_col) * (F32(1.0) / d_row)
    nb = min(128, width)
    blocks = width // nb

    def blk(ref, i, j):
        return ref[i * nb:(i + 1) * nb, j * nb:(j + 1) * nb]

    def dot(a, b, dims):
        return lax.dot_general(a, b, (dims, ((), ())), precision=HIGH, preferred_element_type=F32)

    r_ref[...] = jnp.zeros_like(r_ref)
    inv_ref[...] = jnp.zeros_like(inv_ref)
    for k in range(blocks):
        a = blk(gram_ref, k, k)
        for m in range(k):
            a = a - dot(blk(r_ref, m, k), blk(r_ref, m, k), ((0,), (0,)))
        upper, inv = eliminate(a)
        r_ref[k * nb:(k + 1) * nb, k * nb:(k + 1) * nb] = upper
        inv_ref[k * nb:(k + 1) * nb, k * nb:(k + 1) * nb] = inv
        for j in range(k + 1, blocks):
            a = blk(gram_ref, k, j)
            for m in range(k):
                a = a - dot(blk(r_ref, m, k), blk(r_ref, m, j), ((0,), (0,)))
            r_ref[k * nb:(k + 1) * nb, j * nb:(j + 1) * nb] = dot(inv, a, ((1,), (0,)))
        for j in range(k):
            acc = jnp.zeros((nb, nb), F32)
            for m in range(j, k):
                acc = acc + dot(blk(r_ref, m, k), blk(inv_ref, m, j), ((0,), (0,)))
            inv_ref[k * nb:(k + 1) * nb, j * nb:(j + 1) * nb] = -dot(inv, acc, ((1,), (0,)))
    r_ref[...] = r_ref[...] * d_row
    q_ref[...] = dot(y_ref[...] * (F32(1.0) / d_row), inv_ref[...], ((1,), (1,)))
    y_copy.wait()


def per_device(n_snp, n_samp, genotypes, basis_cols):
    words, snps = genotypes.shape
    width = basis_cols.shape[1]
    rows = PLANES * words
    chunks = 3
    own = snps // n_samp
    bits = log2(n_snp)
    packed = width - width // 4
    vmem = pl.BlockSpec(memory_space=pltpu.VMEM)
    dma = pltpu.SemaphoreType.DMA
    y, gram = pl.pallas_call(
        functools.partial(main_kernel, n_snp, n_samp, chunks),
        out_shape=(
            jax.ShapeDtypeStruct((own, width), F32),
            jax.ShapeDtypeStruct((width, width), F32),
        ),
        in_specs=[vmem, vmem],
        out_specs=(vmem, vmem),
        scratch_shapes=[
            pltpu.VMEM((rows, width), F32),
            pltpu.VMEM((rows, width), F32),
            pltpu.VMEM((rows, width), BF16),
            pltpu.VMEM((snps, rows), BF16),
            pltpu.VMEM((8, width), F32),
            pltpu.VMEM((n_snp, 8, width), F32),
            pltpu.VMEM((8, width), F32),
            pltpu.VMEM((n_samp, 8, width), F32),
            pltpu.VMEM((n_samp, own, width), jnp.int16),
            pltpu.VMEM((n_samp, 8, width), F32),
            pltpu.VMEM((n_samp, own, width), jnp.int16),
            pltpu.VMEM((n_samp, 8, width), F32),
            pltpu.VMEM((packed, width), F32),
            pltpu.VMEM((packed, width), F32),
            pltpu.VMEM((n_samp, packed // n_snp, width), F32),
            pltpu.VMEM((packed, width), F32),
            dma((chunks, bits)), dma((chunks, bits)), dma((chunks, bits)), dma((chunks, bits)),
            dma((n_snp,)), dma((n_snp,)), dma((n_samp,)), dma((n_samp,)),
            dma((n_samp,)), dma((n_samp,)), dma((n_samp,)), dma((n_samp,)),
            dma((bits,)), dma((bits,)), dma((n_samp,)), dma((n_samp,)), dma((bits,)), dma((bits,)),
        ],
        compiler_params=pltpu.CompilerParams(collective_id=0, has_side_effects=True),
    )(genotypes, basis_cols)
    y, r_factor, q_next = pl.pallas_call(
        factor_kernel,
        out_shape=(
            jax.ShapeDtypeStruct((own, width), F32),
            jax.ShapeDtypeStruct((width, width), F32),
            jax.ShapeDtypeStruct((own, width), F32),
        ),
        in_specs=[vmem, vmem],
        out_specs=(pl.BlockSpec(memory_space=pl.ANY), vmem, vmem),
        scratch_shapes=[
            pltpu.VMEM((width, width), F32),
            pltpu.VMEM((width, width), F32),
            pltpu.SemaphoreType.DMA,
        ],
    )(gram, y)
    layout = (1, 1, own, width)
    return (y.reshape(layout), r_factor, q_next.reshape(layout))


def solution(mesh):
    return jax.shard_map(
        functools.partial(per_device, mesh.shape["snp"], mesh.shape["samp"]),
        mesh=mesh,
        in_specs=(P(("grp", "samp"), "snp"), P(("grp", "snp"), None)),
        out_specs=(
            P(("grp", "snp"), "samp", None, None),
            P("grp", None),
            P(("grp", "snp"), "samp", None, None),
        ),
        check_vma=False,
    )
```

```python
import functools
import jax
import jax.numpy as jnp
from jax import lax
from jax.experimental import pallas as pl
from jax.experimental.pallas import tpu as pltpu
from jax.sharding import PartitionSpec as P

PLANES = 6
MESH = pl.DeviceIdType.MESH
F32 = jnp.float32
BF16 = jnp.bfloat16
HIGH = lax.Precision.HIGHEST
LEVELS = 32767.0


def log2(n):
    bits = n.bit_length() - 1
    assert 1 << bits == n
    return bits


def segments(me, bits, rows):
    base, steps = 0, []
    for b in range(bits):
        bit = (me // (1 << b)) % 2
        half = rows >> (b + 1)
        steps.append((base + bit * half, base + (1 - bit) * half, half))
        base = base + bit * half
    return steps


def main_kernel(
    n_snp, n_samp, chunks,
    g_ref, b_ref, y_ref, gram_ref,
    part, rs_rx, scores, dose_t, cs_tx, cs_rx, ct_tx, ct_rx,
    yq, ysc, yq_rx, ysc_rx, gwork, g_rx, gs_rx, gout,
    rs_s, rs_r, ag_s, ag_r, cs_s, cs_r, ct_s, ct_r, yq_s, yq_r, ysc_s, ysc_r,
    gr_s, gr_r, gs_s, gs_r, ga_s, ga_r,
    coded, coded_rx, meta, meta_rx, mt_s, mt_r,
):
    snp, samp = lax.axis_index("snp"), lax.axis_index("samp")
    bits = log2(n_snp)
    words = g_ref.shape[0]
    rows = PLANES * words
    width = b_ref.shape[1]
    crow = rows // chunks
    samples = rows * n_samp

    def copy(src, dst, ssem, rsem, axis, peer):
        return pltpu.make_async_remote_copy(
            src_ref=src, dst_ref=dst, send_sem=ssem, recv_sem=rsem,
            device_id={axis: peer}, device_id_type=MESH,
        )

    def partner(b):
        bit = (snp // (1 << b)) % 2
        return snp + (1 - 2 * bit) * (1 << b)

    barrier = pltpu.get_barrier_semaphore()
    for d in range(1, n_snp):
        pl.semaphore_signal(barrier, inc=1, device_id={"snp": lax.rem(snp + d, n_snp)}, device_id_type=MESH)
    for d in range(1, n_samp):
        pl.semaphore_signal(barrier, inc=1, device_id={"samp": lax.rem(samp + d, n_samp)}, device_id_type=MESH)

    steps = segments(snp, bits, crow)

    def rows_at(c, off, size):
        return pl.ds(pl.multiple_of(c * crow + off, 16), size)

    def rs_copy(c, b):
        keep, send, half = steps[b]
        return copy(
            part.at[rows_at(c, send, half)],
            rs_rx.at[pl.ds(c * crow + crow - 2 * half, half)],
            rs_s.at[c, b], rs_r.at[c, b], "snp", partner(b),
        )

    def code(c, b):
        keep, send, half = steps[b]
        block = part[rows_at(c, send, half), :]
        mean = jnp.sum(block, axis=0, keepdims=True) * F32(1.0 / half)
        block = block - mean
        top = jnp.maximum(jnp.max(jnp.abs(block), axis=0, keepdims=True), F32(1e-30))
        off = c * crow + crow - 2 * half
        coded[pl.ds(off, half), :] = jnp.round(block * (F32(LEVELS) / top)).astype(jnp.int32).astype(jnp.int16)
        meta[c, b, 0:8, :] = jnp.broadcast_to(top * F32(1.0 / LEVELS), (8, width))
        meta[c, b, 8:16, :] = jnp.broadcast_to(mean, (8, width))

    def coded_copies(c, b):
        half = steps[b][2]
        seg = pl.ds(c * crow + crow - 2 * half, half)
        return (
            copy(coded.at[seg], coded_rx.at[seg], rs_s.at[c, b], rs_r.at[c, b], "snp", partner(b)),
            copy(meta.at[c, b], meta_rx.at[c, b], mt_s.at[c, b], mt_r.at[c, b], "snp", partner(b)),
        )

    def ag_copy(c, b):
        keep, send, half = steps[b]
        seg = rows_at(c, keep, half)
        return copy(scores.at[seg], scores.at[seg], ag_s.at[c, b], ag_r.at[c, b], "snp", partner(b))

    per = PLANES // chunks
    colsum = jnp.zeros((8, width), F32)
    for c in range(chunks):
        for t in range(c * per, (c + 1) * per):
            dose = ((g_ref[...] >> (2 * t)) & 3).astype(F32).astype(BF16)
            prod = jnp.dot(dose, b_ref[...], preferred_element_type=F32)
            part[pl.ds(t * words, words), :] = prod
            colsum = colsum + prod.reshape(words // 8, 8, width).sum(axis=0)
        if c == 0:
            pl.semaphore_wait(barrier, n_snp + n_samp - 2)
        rs_copy(c, 0).start()
    cs_tx[...] = colsum

    def cs_copy(d):
        return copy(cs_tx, cs_rx.at[d], cs_s.at[d], cs_r.at[d], "snp", lax.rem(snp + d, n_snp))

    def ct_copy(d):
        return copy(ct_tx, ct_rx.at[d], ct_s.at[d], ct_r.at[d], "samp", lax.rem(samp + d, n_samp))

    for d in range(1, n_snp):
        cs_copy(d).start()

    def reduce_step(b, center=None):
        for c in range(chunks):
            keep, send, half = steps[b]
            seg = rows_at(c, keep, half)
            arrived = pl.ds(c * crow + crow - 2 * half, half)
            if b == 0:
                rs_copy(c, b).wait()
                total = part[seg, :] + rs_rx[arrived, :]
            else:
                for cp in coded_copies(c, b):
                    cp.wait()
                other = coded_rx[arrived, :].astype(jnp.int32).astype(F32) * meta_rx[c, b, 0:1, :]
                total = part[seg, :] + (other + meta_rx[c, b, 8:9, :])
            if b + 1 < bits:
                part[seg, :] = total
                code(c, b + 1)
                for cp in coded_copies(c, b + 1):
                    cp.start()
            else:
                scores[seg, :] = (total - center).astype(BF16)
                ag_copy(c, b).start()

    for b in range(bits - 1):
        reduce_step(b)
        if b == 0:
            tot = colsum
            for d in range(1, n_snp):
                cs_copy(d).wait()
                tot = tot + cs_rx[d]
            ct_tx[...] = tot
            for d in range(1, n_samp):
                ct_copy(d).start()
    word_t = g_ref[...].T
    for t in range(PLANES):
        dose_t[:, t * words:(t + 1) * words] = ((word_t >> (2 * t)) & 3).astype(F32).astype(BF16)
    for d in range(1, n_samp):
        ct_copy(d).wait()
        tot = tot + ct_rx[d]
    center = tot.sum(axis=0, keepdims=True) / F32(samples)
    reduce_step(bits - 1, center)
    for b in range(bits - 1, -1, -1):
        for c in range(chunks):
            ag_copy(c, b).wait()
            if b:
                ag_copy(c, b - 1).start()

    inv_root = F32(1.0) / jnp.sqrt(F32(samples))
    own_rows = y_ref.shape[0]

    def y_part(owner):
        blk = dose_t[pl.ds(pl.multiple_of(owner * own_rows, 16), own_rows), :]
        return jnp.dot(blk, scores[...], preferred_element_type=F32) * inv_root

    def y_copies(d):
        to = lax.rem(samp + d, n_samp)
        return (
            copy(yq.at[d], yq_rx.at[d], yq_s.at[d], yq_r.at[d], "samp", to),
            copy(ysc.at[d], ysc_rx.at[d], ysc_s.at[d], ysc_r.at[d], "samp", to),
        )

    for d in range(1, n_samp):
        block = y_part(lax.rem(samp + d, n_samp))
        top = jnp.maximum(jnp.max(jnp.abs(block), axis=0, keepdims=True), F32(1e-30))
        yq[d] = jnp.round(block * (F32(LEVELS) / top)).astype(jnp.int32).astype(jnp.int16)
        ysc[d] = jnp.broadcast_to(top * F32(1.0 / LEVELS), (8, width))
        for cp in y_copies(d):
            cp.start()
    y = y_part(samp)
    for d in range(1, n_samp):
        for cp in y_copies(d):
            cp.wait()
        y = y + yq_rx[d].astype(jnp.int32).astype(F32) * ysc_rx[d][0:1, :]
    y_ref[...] = y

    snp_total = dose_t.shape[0] * n_snp
    half_w = width // 2
    packed = width - width // 4
    top = lax.dot_general(y[:, :half_w], y, (((0,), (0,)), ((), ())), precision=HIGH, preferred_element_type=F32)
    low = lax.dot_general(y[:, half_w:], y[:, half_w:], (((0,), (0,)), ((), ())), precision=HIGH, preferred_element_type=F32)
    gwork[:half_w, :] = top / F32(snp_total)
    gwork[half_w:, :half_w] = low[:half_w // 2, :] / F32(snp_total)
    gwork[half_w:, half_w:] = low[half_w // 2:, :] / F32(snp_total)
    gsteps = segments(snp, bits, packed)

    def at(off, size):
        return pl.ds(pl.multiple_of(off, 8), size)

    def gr_copy(b):
        keep, send, half = gsteps[b]
        return copy(gwork.at[at(send, half)], g_rx.at[pl.ds(packed - 2 * half, half)], gr_s.at[b], gr_r.at[b], "snp", partner(b))

    def ga_copy(b):
        keep, send, half = gsteps[b]
        return copy(gout.at[at(keep, half)], gout.at[at(keep, half)], ga_s.at[b], ga_r.at[b], "snp", partner(b))

    for b in range(bits):
        keep, send, half = gsteps[b]
        gr_copy(b).start()
        gr_copy(b).wait()
        mine = gwork[at(keep, half), :] + g_rx[pl.ds(packed - 2 * half, half), :]
        gwork[at(keep, half), :] = mine
    keep, send, half = gsteps[bits - 1]

    def gs_copy(d):
        return copy(gwork.at[at(keep, half)], gs_rx.at[samp], gs_s.at[d], gs_r.at[d], "samp", lax.rem(samp + d, n_samp))

    for d in range(1, n_samp):
        gs_copy(d).start()
    gs_rx[samp] = mine
    for d in range(1, n_samp):
        gs_copy(d).wait()
    total = gs_rx[0]
    for j in range(1, n_samp):
        total = total + gs_rx[j]
    gout[at(keep, half), :] = total
    for b in range(bits - 1, -1, -1):
        ga_copy(b).start()
        ga_copy(b).wait()
    gram_ref[:half_w, :] = gout[:half_w, :]
    gram_ref[half_w:half_w + half_w // 2, half_w:] = gout[half_w:, :half_w]
    gram_ref[half_w + half_w // 2:, half_w:] = gout[half_w:, half_w:]
    gram_ref[half_w:, :half_w] = jnp.zeros((half_w, half_w), F32)


def eliminate(a):
    n = a.shape[0]
    groups = n // 8
    lane = lax.broadcasted_iota(jnp.int32, (8, n), 1)
    sub = lax.broadcasted_iota(jnp.int32, (8, n), 0)
    left = [a[8 * g:8 * g + 8, :] for g in range(groups)]
    right = [jnp.where(lane == sub + 8 * g, F32(1.0), F32(0.0)) for g in range(groups)]

    def across(x, j):
        return jnp.broadcast_to(x[:, j:j + 1], (8, n))

    def down(x, s):
        return jnp.broadcast_to(x[s:s + 1, :], (8, n))

    for g0 in range(groups):
        jl, jr = left[g0], right[g0]
        cols = [across(jl, 8 * g0 + i) for i in range(8)]
        up_l, up_r = jl, jr
        for s in range(0, 8, 2):
            c0, c1 = cols[s], cols[s + 1]
            a00, a10, a11 = down(c0, s), down(c0, s + 1), down(c1, s + 1)
            inv_a = F32(1.0) / a00
            inv_det = F32(1.0) / (a00 * a11 - a10 * a10)
            m = a10 * inv_a
            f = a00 * inv_det

            def step(x):
                u, v = down(x, s), down(x, s + 1)
                v = v - m * u
                w1 = v * f
                w0 = u * inv_a - m * w1
                x = x - c0 * w0 - c1 * w1
                return u, v, jnp.where(sub == s, w0, jnp.where(sub == s + 1, w1, x))

            for i in range(s + 2, 8):
                cols[i] = step(cols[i])[2]
            u, v, jl = step(jl)
            up_l = jnp.where(sub == s, u, jnp.where(sub == s + 1, v, up_l))
            u, v, jr = step(jr)
            up_r = jnp.where(sub == s, u, jnp.where(sub == s + 1, v, up_r))
        left[g0], right[g0] = up_l, up_r
        rows_l = [down(jl, i) for i in range(8)]
        rows_r = [down(jr, i) for i in range(8)]
        for g in range(g0 + 1, groups):
            xl, xr = left[g], right[g]
            for i in range(8):
                col = across(left[g], 8 * g0 + i)
                xl = xl - col * rows_l[i]
                xr = xr - col * rows_r[i]
            left[g], right[g] = xl, xr
    ups, invs = [], []
    for g in range(groups):
        diag = jnp.sum(jnp.where(lane == sub + 8 * g, left[g], F32(0.0)), axis=1, keepdims=True)
        scale = F32(1.0) / jnp.sqrt(diag)
        ups.append(jnp.where(lane >= sub + 8 * g, left[g] * scale, F32(0.0)))
        invs.append(right[g] * scale)
    return jnp.concatenate(ups, axis=0), jnp.concatenate(invs, axis=0)


def factor_kernel(gram_in, y_ref, y_out, r_ref, q_ref, inv_ref, gram_ref, y_sem):
    y_copy = pltpu.make_async_copy(y_ref, y_out, y_sem)
    y_copy.start()
    width = gram_in.shape[0]
    on = lax.broadcasted_iota(jnp.int32, (width, width), 0) == lax.broadcasted_iota(jnp.int32, (width, width), 1)
    kept = jnp.where(on, gram_in[...], F32(0.0))
    d_row = jnp.sqrt(jnp.sum(kept, axis=0, keepdims=True))
    d_col = jnp.sqrt(jnp.sum(kept, axis=1, keepdims=True))
    gram_ref[...] = gram_in[...] * (F32(1.0) / d_col) * (F32(1.0) / d_row)
    nb = min(128, width)
    blocks = width // nb

    def blk(ref, i, j):
        return ref[i * nb:(i + 1) * nb, j * nb:(j + 1) * nb]

    def dot(a, b, dims):
        return lax.dot_general(a, b, (dims, ((), ())), precision=HIGH, preferred_element_type=F32)

    r_ref[...] = jnp.zeros_like(r_ref)
    inv_ref[...] = jnp.zeros_like(inv_ref)
    for k in range(blocks):
        a = blk(gram_ref, k, k)
        for m in range(k):
            a = a - dot(blk(r_ref, m, k), blk(r_ref, m, k), ((0,), (0,)))
        upper, inv = eliminate(a)
        r_ref[k * nb:(k + 1) * nb, k * nb:(k + 1) * nb] = upper
        inv_ref[k * nb:(k + 1) * nb, k * nb:(k + 1) * nb] = inv
        for j in range(k + 1, blocks):
            a = blk(gram_ref, k, j)
            for m in range(k):
                a = a - dot(blk(r_ref, m, k), blk(r_ref, m, j), ((0,), (0,)))
            r_ref[k * nb:(k + 1) * nb, j * nb:(j + 1) * nb] = dot(inv, a, ((1,), (0,)))
        for j in range(k):
            acc = jnp.zeros((nb, nb), F32)
            for m in range(j, k):
                acc = acc + dot(blk(r_ref, m, k), blk(inv_ref, m, j), ((0,), (0,)))
            inv_ref[k * nb:(k + 1) * nb, j * nb:(j + 1) * nb] = -dot(inv, acc, ((1,), (0,)))
    r_ref[...] = r_ref[...] * d_row
    q_ref[...] = dot(y_ref[...] * (F32(1.0) / d_row), inv_ref[...], ((1,), (1,)))
    y_copy.wait()


def per_device(n_snp, n_samp, genotypes, basis_cols):
    words, snps = genotypes.shape
    width = basis_cols.shape[1]
    rows = PLANES * words
    chunks = 3
    own = snps // n_samp
    bits = log2(n_snp)
    packed = width - width // 4
    vmem = pl.BlockSpec(memory_space=pltpu.VMEM)
    dma = pltpu.SemaphoreType.DMA
    y, gram = pl.pallas_call(
        functools.partial(main_kernel, n_snp, n_samp, chunks),
        out_shape=(
            jax.ShapeDtypeStruct((own, width), F32),
            jax.ShapeDtypeStruct((width, width), F32),
        ),
        in_specs=[vmem, vmem],
        out_specs=(vmem, vmem),
        scratch_shapes=[
            pltpu.VMEM((rows, width), F32),
            pltpu.VMEM((rows, width), F32),
            pltpu.VMEM((rows, width), BF16),
            pltpu.VMEM((snps, rows), BF16),
            pltpu.VMEM((8, width), F32),
            pltpu.VMEM((n_snp, 8, width), F32),
            pltpu.VMEM((8, width), F32),
            pltpu.VMEM((n_samp, 8, width), F32),
            pltpu.VMEM((n_samp, own, width), jnp.int16),
            pltpu.VMEM((n_samp, 8, width), F32),
            pltpu.VMEM((n_samp, own, width), jnp.int16),
            pltpu.VMEM((n_samp, 8, width), F32),
            pltpu.VMEM((packed, width), F32),
            pltpu.VMEM((packed, width), F32),
            pltpu.VMEM((n_samp, packed // n_snp, width), F32),
            pltpu.VMEM((packed, width), F32),
            dma((chunks, bits)), dma((chunks, bits)), dma((chunks, bits)), dma((chunks, bits)),
            dma((n_snp,)), dma((n_snp,)), dma((n_samp,)), dma((n_samp,)),
            dma((n_samp,)), dma((n_samp,)), dma((n_samp,)), dma((n_samp,)),
            dma((bits,)), dma((bits,)), dma((n_samp,)), dma((n_samp,)), dma((bits,)), dma((bits,)),
            pltpu.VMEM((rows, width), jnp.int16),
            pltpu.VMEM((rows, width), jnp.int16),
            pltpu.VMEM((chunks, bits, 16, width), F32),
            pltpu.VMEM((chunks, bits, 16, width), F32),
            dma((chunks, bits)), dma((chunks, bits)),
        ],
        compiler_params=pltpu.CompilerParams(collective_id=0, has_side_effects=True),
    )(genotypes, basis_cols)
    y, r_factor, q_next = pl.pallas_call(
        factor_kernel,
        out_shape=(
            jax.ShapeDtypeStruct((own, width), F32),
            jax.ShapeDtypeStruct((width, width), F32),
            jax.ShapeDtypeStruct((own, width), F32),
        ),
        in_specs=[vmem, vmem],
        out_specs=(pl.BlockSpec(memory_space=pl.ANY), vmem, vmem),
        scratch_shapes=[
            pltpu.VMEM((width, width), F32),
            pltpu.VMEM((width, width), F32),
            pltpu.SemaphoreType.DMA,
        ],
    )(gram, y)
    layout = (1, 1, own, width)
    return (y.reshape(layout), r_factor, q_next.reshape(layout))


def solution(mesh):
    return jax.shard_map(
        functools.partial(per_device, mesh.shape["snp"], mesh.shape["samp"]),
        mesh=mesh,
        in_specs=(P(("grp", "samp"), "snp"), P(("grp", "snp"), None)),
        out_specs=(
            P(("grp", "snp"), "samp", None, None),
            P("grp", None),
            P(("grp", "snp"), "samp", None, None),
        ),
        check_vma=False,
    )
```
